512 devices in a mesh: fsdp: 16 (over x, y), dp: 32 (over z, core).
Axes of the slice: x: 4, y: 4, z: 16, core: 2. Of those that a mesh axis runs over, the one named last changes fastest.
Arguments:
- tokens: bfloat16 [65536, 4096], P(('fsdp', 'dp')), may hold values from -6 to 6
- master_old: float32 [512, 128, 128], P(('fsdp', 'dp')), may hold values from -0.25 to 0.25
- moment_old: float32 [512, 128, 128], P(('fsdp', 'dp')), may hold values from -6 to 6
- second_old: float32 [512, 128, 128], P(('fsdp', 'dp')), may hold values from 0.01 to 1
- old_cell: int32 [112, 4], P('fsdp'), may hold values from 0 to 31, as said below
- new_cell: int32 [112, 4], P('fsdp'), may hold values from 0 to 31, as said below
- regrown: int32 [112, 4], P('fsdp'), may hold values 0 or 1
- new_rows: int32 [112, 4], replicated, may hold values from 0 to 31, as said below
Outputs:
- hidden: bfloat16 [65536, 14336], P(('fsdp', 'dp'))
- master_new: float32 [512, 128, 128], P(('fsdp', 'dp'))
- moment_new: float32 [512, 128, 128], P(('fsdp', 'dp'))
- second_new: float32 [512, 128, 128], P(('fsdp', 'dp'))
The draws below stay inside these ranges and needn't reach their ends.
Inputs may be any that keep to these rules, and one draw needn't show every extreme that they name: `old_cell`: within one fsdp index, taking its slots column by column and then by k, the old cells strictly increase; a cell's index // 1 is its holder along dp and index % 1 its place in that holder's buffer. `new_cell`: strictly increasing in the same order; every slot's new cell differs from its old cell by at most 4, and by exactly 4 for some slot of every fsdp index. `new_rows`: the 4 block rows of one block column are distinct.
All inputs are finite; a program needn't handle non-finite values. No bound on the sum of `regrown` on one device may be relied on, other than what follows from the above.
Results may differ from the reference program's by a relative error of at most 0.007.
Values may be sent and summed in bfloat16 or wider, within the bound.
No kernel may reach another device: no remote copies, remote signals or barrier semaphores. Data moves between devices by JAX's collectives and lax.ppermute only.
A program may use at most 128 MiB of HBM per device.

```python
import math
import jax
import jax.numpy as jnp
from jax import lax

D = 4096
FF = 14336
BLK = 128
NZC = 4
NBR = 32
NBC = 112
BCF = 7
SLOTS = 28
CELLS = 32
HOLES = 4
STORE = 512
TOKENS = 65536
N_FSDP = 16


def cell_pair(key):
    subkeys = jax.random.split(jax.random.fold_in(key, 11), 4)
    pivot = jax.random.randint(subkeys[0], (N_FSDP, 1, 1), 0, SLOTS)
    raw_old = jax.random.randint(subkeys[1], (N_FSDP, HOLES, 1), 0, 1 << 20)
    raw_new = jax.random.randint(subkeys[2], (N_FSDP, HOLES, 1), 0, 1 << 20)
    cuts_old = pivot + 1 + raw_old % (SLOTS - pivot)
    cuts_new = raw_new % (pivot + 1)
    index = jnp.arange(SLOTS, dtype=jnp.int32)[None, None, :]
    shift_old = jnp.sum((cuts_old <= index).astype(jnp.int32), axis=1)
    shift_new = jnp.sum((cuts_new <= index).astype(jnp.int32), axis=1)
    base = jnp.arange(SLOTS, dtype=jnp.int32)[None, :]
    old_cells = (base + shift_old).astype(jnp.int32)
    new_cells = (base + shift_new).astype(jnp.int32)
    ranking = jax.random.permutation(subkeys[3], N_FSDP)
    mirrored = (ranking < N_FSDP // 2)[:, None]
    old_cells = jnp.where(mirrored, CELLS - 1 - old_cells[:, ::-1], old_cells)
    new_cells = jnp.where(mirrored, CELLS - 1 - new_cells[:, ::-1], new_cells)
    return (old_cells.reshape(NBC, NZC).astype(jnp.int32), new_cells.reshape(NBC, NZC).astype(jnp.int32))


def draw_old_cell(key, part):
    return cell_pair(key)[0]


def draw_new_cell(key, part):
    return cell_pair(key)[1]


def draw_new_rows(key, part):
    subkeys = jax.random.split(jax.random.fold_in(key, 23), NBC)
    picks = jax.vmap(lambda sub: jax.random.permutation(sub, NBR)[:NZC])(subkeys)
    return picks.astype(jnp.int32)


def touch_ends(drawn, own_key, smallest, top_value):
    longest = drawn.shape.index(max(drawn.shape))
    spots = []
    for shift in (0, 1):
        where = [jax.random.randint(jax.random.fold_in(own_key, axis), (), 0, length) for axis, length in enumerate(drawn.shape)]
        where[longest] = (where[longest] + shift) % drawn.shape[longest]
        spots.append(tuple(where))
    return drawn.at[spots[0]].set(smallest).at[spots[1]].set(top_value)


def levels(key, shape, shards, least, top_value):
    factor_of = 1.0
    for dim, shards_of in shards:
        heights = jax.random.uniform(jax.random.fold_in(jax.random.fold_in(key, 6), dim), (shards_of,), jnp.float32, least / len(shards), top_value / len(shards))
        factor_of = factor_of * jnp.repeat(jnp.exp(heights), shape[dim] // shards_of).reshape((-1,) + (1,) * (len(shape) - 1 - dim))
    return factor_of


def noise(stream_key, dims, deviation, limit, cuts=(), held_as=jnp.bfloat16):
    array = deviation * jax.random.normal(stream_key, dims, jnp.float32)
    if cuts:
        array = array * levels(stream_key, dims, cuts, -0.22, 0.18)
    return jnp.clip(array, -limit, limit).astype(held_as)


def setup_inputs(seed: int = 0) -> dict:
    key_list = jax.random.split(jax.random.key(seed), 9)
    return {
        "tokens": noise(key_list[0], (TOKENS, D), 1.0, 6.0, ((0, 512),)),
        "master_old": noise(key_list[1], (STORE, BLK, BLK), (NZC * BLK) ** -0.5, 0.25, ((0, 512),), jnp.float32),
        "moment_old": noise(key_list[2], (STORE, BLK, BLK), 1.0, 6.0, ((0, 512),), jnp.float32),
        "second_old": jnp.clip(jnp.exp(math.log(1.0) - 4.6051702 * jax.random.uniform(key_list[3], (STORE, BLK, BLK), jnp.float32) ** levels(key_list[3], (STORE, BLK, BLK), ((0, 512),), -0.2, 0.2)), 0.01, 1.0),
        "old_cell": draw_old_cell(jax.random.fold_in(key_list[8], 71), 0),
        "new_cell": draw_new_cell(jax.random.fold_in(key_list[8], 71), 0),
        "regrown": touch_ends((jax.random.randint(key_list[6], (NBC, NZC), 0, 10) < 3).astype(jnp.int32), jax.random.fold_in(key_list[6], 1), 0, 1),
        "new_rows": draw_new_rows(jax.random.fold_in(key_list[8], 71), 0),
    }


def reference(tokens, master_old, moment_old, second_old, old_cell, new_cell, regrown, new_rows):
    groups = (jnp.arange(NBC, dtype=jnp.int32) // BCF).astype(jnp.int32)
    old_place = (groups[:, None] * CELLS + old_cell).reshape(-1).astype(jnp.int32)
    new_place = (groups[:, None] * CELLS + new_cell).reshape(-1).astype(jnp.int32)
    keep_flag = (regrown.reshape(-1) == 0)

    def migrate(buffer):
        moved = jnp.where(keep_flag[:, None, None], buffer[old_place], jnp.zeros((), buffer.dtype))
        placed = jnp.zeros_like(buffer).at[new_place].set(moved)
        return moved, placed

    master_moved, master_new = migrate(master_old)
    moment_moved, moment_new = migrate(moment_old)
    second_moved, second_new = migrate(second_old)
    weight_block = master_moved.astype(jnp.bfloat16).reshape(NBC, NZC, BLK, BLK)
    token_blocks = tokens.reshape(TOKENS, NBR, BLK)

    def column(inputs):
        row_index, block_set = inputs
        picked = jnp.take(token_blocks, row_index.astype(jnp.int32), axis=1).reshape(TOKENS, NZC * BLK)
        product = jnp.dot(picked, block_set.reshape(NZC * BLK, BLK), preferred_element_type=jnp.float32)
        return product.astype(jnp.bfloat16)

    stacked = lax.map(column, (new_rows, weight_block))
    hidden = jnp.transpose(stacked, (1, 0, 2)).reshape(TOKENS, FF)
    return hidden, master_new, moment_new, second_new
```

```python
import numpy as np
import jax
import jax.numpy as jnp
from jax import lax
from jax.experimental import pallas as pl
from jax.experimental.pallas import tpu as pltpu
from jax.sharding import Mesh, PartitionSpec as P

BF = jnp.bfloat16
F32 = jnp.float32
X, Y, Z, C = 4, 4, 16, 2
G = X * Y
B = 128
COLS = 7
K = 4
MINE = 14
T = 128
ALL = ("x", "y", "z", "core")
VMEM = pl.BlockSpec(memory_space=pltpu.VMEM)
SMEM = pl.BlockSpec(memory_space=pltpu.SMEM)
PARAMS = pltpu.CompilerParams(vmem_limit_bytes=48 << 20)


def device(x, y, z, c):
    return ((x * Y + y) * Z + z) * C + c


def line_groups(first):
    out = []
    for c in range(C):
        for z in range(Z):
            for o in range(4):
                along_x = (c == 0) == first
                out.append([device(i, o, z, c) if along_x else device(o, i, z, c) for i in range(4)])
    return out


def slot_of(c, j):
    return (3 * c + j // K, j % K) if j < 12 else (COLS - 1, 2 * c + j - 12)


def group_at(c, i):
    return jnp.where(c == 0, (i % 4) * 4 + i // 4, i)


def prep_kernel(place, old, new, regrown, master, block, info):
    cell = place[0]
    above, below = (cell + 1) % (Z * C), (cell - 1) % (Z * C)

    def look(s, carry):
        kept, o0, k0, op, om = carry
        o, n, r = old[s % K, s // K], new[s % K, s // K], regrown[s % K, s // K]
        kept = jnp.where((o == cell) & (r == 0), 1, kept)
        k0 = jnp.where((n == cell) & (r == 0), 1, k0)
        o0 = jnp.where(n == cell, o, o0)
        op = jnp.where(n == above, o, op)
        om = jnp.where(n == below, o, om)
        return kept, o0, k0, op, om

    kept, o0, k0, op, om = lax.fori_loop(
        0, COLS * K, look, (jnp.int32(0), cell, jnp.int32(0), above, below), unroll=True
    )

    def split(d):
        a = (d + 1 > 1).astype(jnp.int32) * (d > 1).astype(jnp.int32) - (d < -1).astype(jnp.int32)
        return a, d - 3 * a

    a0, b0 = split(cell - o0)
    ap, _ = split(above - op)
    am, _ = split(below - om)
    info[0] = k0
    info[1] = a0
    info[2] = b0
    info[3] = ap
    info[4] = am
    block[0] = jnp.where(kept == 1, master[0], 0.0).astype(BF)


def middle_kernel(info, own, low, high, up, down):
    for out, at in ((up, 3), (down, 4)):
        a = info[at]
        out[...] = jnp.where(a == 0, own[...], jnp.where(a == 1, low[...], high[...]))


def settle_kernel(info, master, moment, second, low, high, below, above, *outs):
    keep, a, b = info[0], info[1], info[2]
    for m, (own, out) in enumerate(zip((master, moment, second), outs)):
        same = jnp.where(a == 0, own[0], jnp.where(a == 1, low[m], high[m]).astype(F32))
        moved = jnp.where(b == 1, below[m], above[m]).astype(F32)
        value = jnp.where(b == 0, same, moved)
        out[0] = jnp.where(keep == 1, value, 0.0)


def pick_kernel(place, old, own, other, out):
    c = place[1]
    for j in range(MINE):
        if j < 12:
            o = old[j % K, 3 * c + j // K]
        else:
            o = old[2 * c + j - 12, COLS - 1]
        at = o // 2
        block = jnp.where(o % 2 == c, own[at], other[at])
        for t in range(4):
            out[t, j] = block


def product_kernel(place, rows, mine, theirs, blocks, own3, own6, send):
    c = place[1]

    def group(i, _):
        f = group_at(c, i)
        for j in range(4):
            col = f * COLS + (3 * c + j if j < 3 else COLS - 1)
            count = K if j < 3 else 2
            ks = [k if j < 3 else 2 * c + k for k in range(count)]
            at = [pl.multiple_of(rows[k, col] * B, B) for k in ks]
            left = jnp.concatenate(
                [jnp.concatenate([ref[:, pl.ds(p, B)] for p in at], axis=1) for ref in (mine, theirs)], axis=0
            )
            right = blocks[pl.ds(i * MINE + j * K, count)].reshape(count * B, B)
            acc = jnp.dot(left, right, preferred_element_type=F32)
            if j < 3:
                own3[:, pl.ds(pl.multiple_of(i * 384 + j * B, B), B)] = acc[:T].astype(BF)
            else:
                own6[:, pl.ds(pl.multiple_of(i * B, B), B)] = acc[:T]
            send[:, pl.ds(pl.multiple_of(i * 512 + j * B, B), B)] = acc[T:].astype(BF)
        return 0

    lax.fori_loop(0, G, group, 0)


def join_kernel(place, own3, own6, got, out):
    c = place[1]
    for t in range(4):
        f = pl.program_id(0) * 4 + t
        turned = (f % 4) * 4 + f // 4
        i = jnp.where(c == 0, turned, f)
        o = jnp.where(c == 0, f, turned)
        base = t * COLS * B
        out[:, pl.ds(pl.multiple_of(base + c * 384, B), 384)] = own3[:, pl.ds(pl.multiple_of(i * 384, B), 384)]
        out[:, pl.ds(pl.multiple_of(base + (1 - c) * 384, B), 384)] = got[:, pl.ds(pl.multiple_of(o * 512, B), 384)]
        last = own6[:, pl.ds(pl.multiple_of(i * B, B), B)]
        last = last + got[:, pl.ds(pl.multiple_of(o * 512 + 384, B), B)].astype(F32)
        out[:, base + 768 : base + 896] = last.astype(BF)


def gather(blocks, groups):
    return lax.all_to_all(blocks, ALL, 0, 0, tiled=True, axis_index_groups=groups)


def to_sibling(value):
    return lax.ppermute(value, "core", [(0, 1), (1, 0)])


def along_cells(value, distance):
    route = [(i, (i + distance) % (Z * C)) for i in range(Z * C)]
    return lax.ppermute(value, ("z", "core"), route)


def call(kernel, shapes, in_specs, out_specs, name, **more):
    out = [jax.ShapeDtypeStruct(s, d) for s, d in shapes]
    return pl.pallas_call(
        kernel, out_shape=out, in_specs=in_specs, out_specs=out_specs, name=name, compiler_params=PARAMS, **more
    )


def on_device(tokens, master, moment, second, old_cell, new_cell, regrown, new_rows):
    c = lax.axis_index("core")
    cell = lax.axis_index("z") * C + c
    place = jnp.stack([cell, c]).astype(jnp.int32)
    theirs = to_sibling(tokens)
    old_cell, new_cell, regrown = old_cell.T, new_cell.T, regrown.T
    block, info = call(
        prep_kernel, [((1, B, B), BF), ((8,), jnp.int32)], [SMEM] * 4 + [VMEM], [VMEM, SMEM], "prep"
    )(place, old_cell, new_cell, regrown, master)
    own = lax.all_gather(block, "z", axis=0, tiled=True)
    other = to_sibling(own)
    (picked,) = call(pick_kernel, [((4, MINE, B, B), BF)], [SMEM, SMEM, VMEM, VMEM], [VMEM], "pick")(
        place, old_cell, own, other
    )
    line = gather(picked, line_groups(True)).reshape(4 * MINE, B, B)
    line, master, moment, second = lax.optimization_barrier((line, master, moment, second))
    load = jnp.concatenate([master, moment, second]).astype(BF)
    low = along_cells(load, 3)
    high = along_cells(load, -3)
    up, down = call(middle_kernel, [((3, B, B), BF)] * 2, [SMEM] + [VMEM] * 3, [VMEM] * 2, "middle")(
        info, load, low, high
    )
    below = along_cells(up, 1)
    above = along_cells(down, -1)
    wide = jnp.broadcast_to(line[None], (4, 4 * MINE, B, B))
    blocks = gather(wide, line_groups(False)).reshape(G * MINE, B, B)
    states = call(settle_kernel, [((1, B, B), F32)] * 3, [SMEM] + [VMEM] * 7, [VMEM] * 3, "settle")(
        info, master, moment, second, low, high, below, above
    )
    tokens, theirs, states = lax.optimization_barrier((tokens, theirs, tuple(states)))
    own3, own6, send = call(
        product_kernel,
        [((T, G * 384), BF), ((T, G * B), F32), ((T, G * 512), BF)],
        [SMEM, SMEM, VMEM, VMEM, VMEM],
        [VMEM] * 3,
        "product",
    )(place, new_rows.T, tokens, theirs, blocks)
    got = to_sibling(send)
    (hidden,) = call(
        join_kernel,
        [((T, G * COLS * B), BF)],
        [SMEM, VMEM, VMEM, VMEM],
        [pl.BlockSpec((T, 4 * COLS * B), lambda g: (0, g))],
        "join",
        grid=(4,),
    )(place, own3, own6, got)
    return (hidden, *states)


def solution(mesh):
    fine = Mesh(np.asarray(mesh.devices).reshape(X, Y, Z, C), ALL)
    return jax.shard_map(
        on_device,
        mesh=fine,
        in_specs=(P(ALL, None),) + (P(ALL, None, None),) * 3 + (P(("x", "y"), None),) * 3 + (P(),),
        out_specs=(P(ALL, None),) + (P(ALL, None, None),) * 3,
        check_vma=False,
    )
```

```python
import functools
import numpy as np
import jax
import jax.numpy as jnp
from jax import lax
from jax.experimental import pallas as pl
from jax.experimental.pallas import tpu as pltpu
from jax.sharding import Mesh, PartitionSpec as P

BF = jnp.bfloat16
F32 = jnp.float32
X, Y, Z, C = 4, 4, 16, 2
G = X * Y
B = 128
COLS = 7
K = 4
MINE = 14
T = 128
ALL = ("x", "y", "z", "core")
VMEM = pl.BlockSpec(memory_space=pltpu.VMEM)
SMEM = pl.BlockSpec(memory_space=pltpu.SMEM)
ANY = pl.BlockSpec(memory_space=pl.ANY)
PARAMS = pltpu.CompilerParams(vmem_limit_bytes=48 << 20)


def device(x, y, z, c):
    return ((x * Y + y) * Z + z) * C + c


def line_groups(first):
    out = []
    for c in range(C):
        for z in range(Z):
            for o in range(4):
                along_x = (c == 0) == first
                out.append([device(i, o, z, c) if along_x else device(o, i, z, c) for i in range(4)])
    return out


PARTS = {"early": ((0, 0), (3, 0), (1, 0)), "opposite": ((2, 0), (2, 2))}
STEPS = {"early": 4, "opposite": 2}


def group_at(place, c, shift, q):
    line = (jnp.where(c == 0, place[3], place[2]) + shift) % 4
    return jnp.where(c == 0, q * 4 + line, line * 4 + q)


def prep_kernel(place, old, new, regrown, master, block, info):
    cell = place[0]
    above, below = (cell + 1) % (Z * C), (cell - 1) % (Z * C)

    def look(s, carry):
        kept, o0, k0, op, om = carry
        o, n, r = old[s % K, s // K], new[s % K, s // K], regrown[s % K, s // K]
        kept = jnp.where((o == cell) & (r == 0), 1, kept)
        k0 = jnp.where((n == cell) & (r == 0), 1, k0)
        o0 = jnp.where(n == cell, o, o0)
        op = jnp.where(n == above, o, op)
        om = jnp.where(n == below, o, om)
        return kept, o0, k0, op, om

    kept, o0, k0, op, om = lax.fori_loop(
        0, COLS * K, look, (jnp.int32(0), cell, jnp.int32(0), above, below), unroll=True
    )

    def split(d):
        a = (d + 1 > 1).astype(jnp.int32) * (d > 1).astype(jnp.int32) - (d < -1).astype(jnp.int32)
        return a, d - 3 * a

    a0, b0 = split(cell - o0)
    ap, _ = split(above - op)
    am, _ = split(below - om)
    info[0] = k0
    info[1] = a0
    info[2] = b0
    info[3] = ap
    info[4] = am
    block[0] = jnp.where(kept == 1, master[0], 0.0).astype(BF)


def middle_kernel(info, own, low, high, up, down):
    for out, at in ((up, 3), (down, 4)):
        a = info[at]
        out[...] = jnp.where(a == 0, own[...], jnp.where(a == 1, low[...], high[...]))


def settle_kernel(info, master, moment, second, low, high, below, above, *outs):
    keep, a, b = info[0], info[1], info[2]
    for m, (own, out) in enumerate(zip((master, moment, second), outs)):
        same = jnp.where(a == 0, own[0], jnp.where(a == 1, low[m], high[m]).astype(F32))
        moved = jnp.where(b == 1, below[m], above[m]).astype(F32)
        value = jnp.where(b == 0, same, moved)
        out[0] = jnp.where(keep == 1, value, 0.0)


def pick_kernel(place, old, own, other, out):
    c = place[1]
    for j in range(MINE):
        if j < 12:
            o = old[j % K, 3 * c + j // K]
        else:
            o = old[2 * c + j - 12, COLS - 1]
        at = o // 2
        block = jnp.where(o % 2 == c, own[at], other[at])
        for t in range(4):
            out[t, j] = block


def product_kernel(part, place, rows, mine, theirs, *refs):
    layout, steps = PARTS[part], STEPS[part]
    given, refs = refs[: len(layout)], refs[len(layout) :]
    hidden, send, own6, stage, sem = refs[-5:]
    c = place[1]
    step = pl.program_id(0)

    def copy_out(n, s):
        shift, first = layout[n]
        i = n * steps + s
        col = group_at(place, c, shift, first + s) * COLS + 3 * c
        to = hidden.at[:, pl.ds(pl.multiple_of(col * B, B), 3 * B)]
        return pltpu.make_async_copy(stage.at[i], to, sem.at[i])

    for n, (shift, first) in enumerate(layout):
        i = n * steps + step
        f = group_at(place, c, shift, first + step)
        for j in range(4):
            col = f * COLS + (3 * c + j if j < 3 else COLS - 1)
            count = K if j < 3 else 2
            ks = [k if j < 3 else 2 * c + k for k in range(count)]
            at = [pl.multiple_of(rows[k, col] * B, B) for k in ks]
            left = jnp.concatenate(
                [jnp.concatenate([ref[:, pl.ds(p, B)] for p in at], axis=1) for ref in (mine, theirs)], axis=0
            )
            right = given[n][j * K : j * K + count].reshape(count * B, B)
            acc = jnp.dot(left, right, preferred_element_type=F32)
            if j < 3:
                stage[i, :, j * B : j * B + B] = acc[:T].astype(BF)
            else:
                own6[i] = acc[:T]
            send[:, pl.ds(pl.multiple_of(i * 512 + j * B, B), B)] = acc[T:].astype(BF)
        copy_out(n, step).start()

    @pl.when(step == steps - 1)
    def _():
        for n in range(len(layout)):
            for s in range(steps):
                copy_out(n, s).wait()


def join_kernel(parts, last, *refs):
    refs = list(refs)
    place = refs.pop(0)
    got = {part: refs.pop(0) for part in (PARTS if last else parts)}
    own6 = {part: refs.pop(0) for part in PARTS} if last else {}
    refs.pop(0)
    hidden = refs.pop(0)
    sem = refs.pop()
    c = place[1]

    def items(part):
        for n, (shift, first) in enumerate(PARTS[part]):
            for s in range(STEPS[part]):
                yield n * STEPS[part] + s, shift, first + s

    copies = []

    def put(source, f, col, width):
        to = hidden.at[:, pl.ds(pl.multiple_of((f * COLS + col) * B, B), width)]
        copies.append(pltpu.make_async_copy(source, to, sem.at[len(copies)]))
        copies[-1].start()

    for part in parts:
        for i, shift, q in items(part):
            put(got[part].at[:, i * 512 : i * 512 + 384], group_at(place, 1 - c, shift, q), 3 * (1 - c), 384)
    if last:
        total, stage = refs
        for part in PARTS:
            for i, shift, q in items(part):
                total[group_at(place, c, shift, q)] = own6[part][i]
        for part in PARTS:
            for i, shift, q in items(part):
                f = group_at(place, 1 - c, shift, q)
                stage[f] = (total[f] + got[part][:, i * 512 + 384 : i * 512 + 512].astype(F32)).astype(BF)
                put(stage.at[f], f, COLS - 1, B)
    for copy in copies:
        copy.wait()


def gather(blocks, groups):
    return lax.all_to_all(blocks, ALL, 0, 0, tiled=True, axis_index_groups=groups)


def along_ring(value, distance):
    route = [(ring[i], ring[(i + distance) % 4]) for ring in line_groups(False) for i in range(4)]
    return lax.ppermute(value, ALL, route)


def to_sibling(value):
    return lax.ppermute(value, "core", [(0, 1), (1, 0)])


def along_cells(value, distance):
    route = [(i, (i + distance) % (Z * C)) for i in range(Z * C)]
    return lax.ppermute(value, ("z", "core"), route)


def call(kernel, shapes, in_specs, out_specs, name, **more):
    out = [jax.ShapeDtypeStruct(s, d) for s, d in shapes]
    return pl.pallas_call(
        kernel, out_shape=out, in_specs=in_specs, out_specs=out_specs, name=name, compiler_params=PARAMS, **more
    )


def product(part, place, rows, mine, theirs, given, hidden):
    count = len(given) * STEPS[part]
    whole = lambda s: pl.BlockSpec(s, lambda g: (0,) * len(s))
    args = [place, rows, mine, theirs, *given] + ([] if hidden is None else [hidden])
    return call(
        functools.partial(product_kernel, part),
        [((T, G * COLS * B), BF), ((T, count * 512), BF), ((count, T, B), F32)],
        [SMEM, SMEM, whole(mine.shape), whole(theirs.shape)]
        + [pl.BlockSpec((MINE, B, B), lambda g: (g, 0, 0))] * len(given)
        + ([] if hidden is None else [ANY]),
        [ANY, whole((T, count * 512)), whole((count, T, B))],
        "product_" + part,
        grid=(STEPS[part],),
        cost_estimate=pl.CostEstimate(
            flops=count * MINE * 2 * B * B * 2 * T, bytes_accessed=count * (MINE * B * B * 2 + T * B * 20), transcendentals=0
        ),
        scratch_shapes=[pltpu.VMEM((count, T, 384), BF), pltpu.SemaphoreType.DMA((count,))],
        input_output_aliases={} if hidden is None else {len(args) - 1: 0},
    )(*args)


def join(parts, place, got, own6, hidden):
    args = [place, *got, *own6, hidden]
    count = sum(len(PARTS[p]) * STEPS[p] for p in parts) + (G if own6 else 0)
    stage = [pltpu.VMEM((G, T, B), F32), pltpu.VMEM((G, T, B), BF)] if own6 else []
    return call(
        functools.partial(join_kernel, parts, bool(own6)),
        [(hidden.shape, BF)],
        [SMEM] + [VMEM] * (len(args) - 2) + [ANY],
        [ANY],
        "join_" + parts[-1],
        scratch_shapes=stage + [pltpu.SemaphoreType.DMA((count,))],
        input_output_aliases={len(args) - 1: 0},
    )(*args)[0]


def on_device(tokens, master, moment, second, old_cell, new_cell, regrown, new_rows):
    c = lax.axis_index("core")
    cell = lax.axis_index("z") * C + c
    place = jnp.stack([cell, c, lax.axis_index("x"), lax.axis_index("y")]).astype(jnp.int32)
    rows = new_rows.T
    old_cell, new_cell, regrown = old_cell.T, new_cell.T, regrown.T
    block, info = call(
        prep_kernel, [((1, B, B), BF), ((8,), jnp.int32)], [SMEM] * 4 + [VMEM], [VMEM, SMEM], "prep"
    )(place, old_cell, new_cell, regrown, master)
    own = lax.all_gather(block, "z", axis=0, tiled=True)
    other = to_sibling(own)
    (picked,) = call(pick_kernel, [((4, MINE, B, B), BF)], [SMEM, SMEM, VMEM, VMEM], [VMEM], "pick")(
        place, old_cell, own, other
    )
    line = gather(picked, line_groups(True)).reshape(4 * MINE, B, B)
    line, master, moment, second, tokens = lax.optimization_barrier((line, master, moment, second, tokens))
    lower, upper = along_ring(line, 1), along_ring(line, -1)
    theirs = to_sibling(tokens)
    load = jnp.concatenate([master, moment, second]).astype(BF)
    low = along_cells(load, 3)
    high = along_cells(load, -3)
    up, down = call(middle_kernel, [((3, B, B), BF)] * 2, [SMEM] + [VMEM] * 3, [VMEM] * 2, "middle")(
        info, load, low, high
    )
    below = along_cells(up, 1)
    above = along_cells(down, -1)
    lower, upper, below, above = lax.optimization_barrier((lower, upper, below, above))
    states = call(settle_kernel, [((1, B, B), F32)] * 3, [SMEM] + [VMEM] * 7, [VMEM] * 3, "settle")(
        info, master, moment, second, low, high, below, above
    )
    half = 2 * MINE
    go_up, go_down, tokens = lax.optimization_barrier((lower[:half], upper[half:], tokens))
    over = [along_ring(go_up, 1), along_ring(go_down, -1)]
    hidden, send, own6_early = product("early", place, rows, tokens, theirs, [line, lower, upper], None)
    send, over = lax.optimization_barrier((send, over))
    got_early = to_sibling(send)
    hidden, send, own6_opposite = product("opposite", place, rows, tokens, theirs, over, hidden)
    got_opposite = to_sibling(send)
    hidden = join(("early",), place, (got_early,), (), hidden)
    hidden = join(("opposite",), place, (got_early, got_opposite), (own6_early, own6_opposite), hidden)
    return (hidden, *states)


def solution(mesh):
    fine = Mesh(np.asarray(mesh.devices).reshape(X, Y, Z, C), ALL)
    return jax.shard_map(
        on_device,
        mesh=fine,
        in_specs=(P(ALL, None),) + (P(ALL, None, None),) * 3 + (P(("x", "y"), None),) * 3 + (P(),),
        out_specs=(P(ALL, None),) + (P(ALL, None, None),) * 3,
        check_vma=False,
    )
```

```python
import functools
import numpy as np
import jax
import jax.numpy as jnp
from jax import lax
from jax.experimental import pallas as pl
from jax.experimental.pallas import tpu as pltpu
from jax.sharding import Mesh, PartitionSpec as P

BF = jnp.bfloat16
F32 = jnp.float32
X, Y, Z, C = 4, 4, 16, 2
G = X * Y
B = 128
COLS = 7
K = 4
MINE = 14
T = 128
ALL = ("x", "y", "z", "core")
VMEM = pl.BlockSpec(memory_space=pltpu.VMEM)
SMEM = pl.BlockSpec(memory_space=pltpu.SMEM)
ANY = pl.BlockSpec(memory_space=pl.ANY)
PARAMS = pltpu.CompilerParams(vmem_limit_bytes=48 << 20)


def device(x, y, z, c):
    return ((x * Y + y) * Z + z) * C + c


def line_groups(first):
    out = []
    for c in range(C):
        for z in range(Z):
            for o in range(4):
                along_x = (c == 0) == first
                out.append([device(i, o, z, c) if along_x else device(o, i, z, c) for i in range(4)])
    return out


PARTS = {
    "early": ((0, 0), (0, 2), (3, 0), (3, 2), (1, 0), (1, 2)),
    "opposite": ((2, 0), (2, 2)),
}
STEPS = {"early": 2, "opposite": 2}


def group_at(place, c, shift, q):
    line = (jnp.where(c == 0, place[3], place[2]) + shift) % 4
    return jnp.where(c == 0, q * 4 + line, line * 4 + q)


def prep_kernel(place, old, new, regrown, master, block, info):
    cell = place[0]
    above, below = (cell + 1) % (Z * C), (cell - 1) % (Z * C)

    def look(s, carry):
        kept, o0, k0, op, om = carry
        o, n, r = old[s % K, s // K], new[s % K, s // K], regrown[s % K, s // K]
        kept = jnp.where((o == cell) & (r == 0), 1, kept)
        k0 = jnp.where((n == cell) & (r == 0), 1, k0)
        o0 = jnp.where(n == cell, o, o0)
        op = jnp.where(n == above, o, op)
        om = jnp.where(n == below, o, om)
        return kept, o0, k0, op, om

    kept, o0, k0, op, om = lax.fori_loop(
        0, COLS * K, look, (jnp.int32(0), cell, jnp.int32(0), above, below), unroll=True
    )

    def split(d):
        a = (d + 1 > 1).astype(jnp.int32) * (d > 1).astype(jnp.int32) - (d < -1).astype(jnp.int32)
        return a, d - 3 * a

    a0, b0 = split(cell - o0)
    ap, _ = split(above - op)
    am, _ = split(below - om)
    info[0] = k0
    info[1] = a0
    info[2] = b0
    info[3] = ap
    info[4] = am
    block[0] = jnp.where(kept == 1, master[0], 0.0).astype(BF)


def middle_kernel(info, own, low, high, up, down):
    for out, at in ((up, 3), (down, 4)):
        a = info[at]
        out[...] = jnp.where(a == 0, own[...], jnp.where(a == 1, low[...], high[...]))


def settle_kernel(info, master, moment, second, low, high, below, above, *outs):
    keep, a, b = info[0], info[1], info[2]
    for m, (own, out) in enumerate(zip((master, moment, second), outs)):
        same = jnp.where(a == 0, own[0], jnp.where(a == 1, low[m], high[m]).astype(F32))
        moved = jnp.where(b == 1, below[m], above[m]).astype(F32)
        value = jnp.where(b == 0, same, moved)
        out[0] = jnp.where(keep == 1, value, 0.0)


def pick_kernel(place, old, own, other, out):
    c = place[1]
    for j in range(MINE):
        if j < 12:
            o = old[j % K, 3 * c + j // K]
        else:
            o = old[2 * c + j - 12, COLS - 1]
        at = o // 2
        block = jnp.where(o % 2 == c, own[at], other[at])
        for t in range(4):
            out[t, j] = block


def product_kernel(part, place, rows, mine, theirs, *refs):
    layout, steps = PARTS[part], STEPS[part]
    given, refs = refs[: len(layout)], refs[len(layout) :]
    hidden, send, own6, stage, sem = refs[-5:]
    c = place[1]
    step = pl.program_id(0)

    def copy_out(n, s):
        shift, first = layout[n]
        i = n * steps + s
        col = group_at(place, c, shift, first + s) * COLS + 3 * c
        to = hidden.at[:, pl.ds(pl.multiple_of(col * B, B), 3 * B)]
        return pltpu.make_async_copy(stage.at[i], to, sem.at[i])

    for n, (shift, first) in enumerate(layout):
        i = n * steps + step
        f = group_at(place, c, shift, first + step)
        for j in range(4):
            col = f * COLS + (3 * c + j if j < 3 else COLS - 1)
            count = K if j < 3 else 2
            ks = [k if j < 3 else 2 * c + k for k in range(count)]
            at = [pl.multiple_of(rows[k, col] * B, B) for k in ks]
            left = jnp.concatenate(
                [jnp.concatenate([ref[:, pl.ds(p, B)] for p in at], axis=1) for ref in (mine, theirs)], axis=0
            )
            right = given[n][j * K : j * K + count].reshape(count * B, B)
            acc = jnp.dot(left, right, preferred_element_type=F32)
            if j < 3:
                stage[i, :, j * B : j * B + B] = acc[:T].astype(BF)
            else:
                own6[i] = acc[:T]
            send[:, pl.ds(pl.multiple_of(i * 512 + j * B, B), B)] = acc[T:].astype(BF)
        copy_out(n, step).start()

    @pl.when(step == steps - 1)
    def _():
        for n in range(len(layout)):
            for s in range(steps):
                copy_out(n, s).wait()


def join_kernel(parts, last, *refs):
    refs = list(refs)
    place = refs.pop(0)
    got = {part: refs.pop(0) for part in (PARTS if last else parts)}
    own6 = {part: refs.pop(0) for part in PARTS} if last else {}
    refs.pop(0)
    hidden = refs.pop(0)
    sem = refs.pop()
    c = place[1]

    def items(part):
        for n, (shift, first) in enumerate(PARTS[part]):
            for s in range(STEPS[part]):
                yield n * STEPS[part] + s, shift, first + s

    copies = []

    def put(source, f, col, width):
        to = hidden.at[:, pl.ds(pl.multiple_of((f * COLS + col) * B, B), width)]
        copies.append(pltpu.make_async_copy(source, to, sem.at[len(copies)]))
        copies[-1].start()

    for part in parts:
        for i, shift, q in items(part):
            put(got[part].at[:, i * 512 : i * 512 + 384], group_at(place, 1 - c, shift, q), 3 * (1 - c), 384)
    if last:
        total, stage = refs
        for part in PARTS:
            for i, shift, q in items(part):
                total[group_at(place, c, shift, q)] = own6[part][i]
        for part in PARTS:
            for i, shift, q in items(part):
                f = group_at(place, 1 - c, shift, q)
                stage[f] = (total[f] + got[part][:, i * 512 + 384 : i * 512 + 512].astype(F32)).astype(BF)
                put(stage.at[f], f, COLS - 1, B)
    for copy in copies:
        copy.wait()


def gather(blocks, groups):
    return lax.all_to_all(blocks, ALL, 0, 0, tiled=True, axis_index_groups=groups)


def along_ring(value, distance):
    route = [(ring[i], ring[(i + distance) % 4]) for ring in line_groups(False) for i in range(4)]
    return lax.ppermute(value, ALL, route)


def to_sibling(value):
    return lax.ppermute(value, "core", [(0, 1), (1, 0)])


def along_cells(value, distance):
    route = [(i, (i + distance) % (Z * C)) for i in range(Z * C)]
    return lax.ppermute(value, ("z", "core"), route)


def call(kernel, shapes, in_specs, out_specs, name, **more):
    out = [jax.ShapeDtypeStruct(s, d) for s, d in shapes]
    return pl.pallas_call(
        kernel, out_shape=out, in_specs=in_specs, out_specs=out_specs, name=name, compiler_params=PARAMS, **more
    )


def product(part, place, rows, mine, theirs, given, hidden):
    count = len(given) * STEPS[part]
    whole = lambda s: pl.BlockSpec(s, lambda g: (0,) * len(s))
    args = [place, rows, mine, theirs, *given] + ([] if hidden is None else [hidden])
    return call(
        functools.partial(product_kernel, part),
        [((T, G * COLS * B), BF), ((T, count * 512), BF), ((count, T, B), F32)],
        [SMEM, SMEM, whole(mine.shape), whole(theirs.shape)]
        + [pl.BlockSpec((MINE, B, B), lambda g: (g, 0, 0))] * len(given)
        + ([] if hidden is None else [ANY]),
        [ANY, whole((T, count * 512)), whole((count, T, B))],
        "product_" + part,
        grid=(STEPS[part],),
        cost_estimate=pl.CostEstimate(
            flops=count * MINE * 2 * B * B * 2 * T, bytes_accessed=count * (MINE * B * B * 2 + T * B * 20), transcendentals=0
        ),
        scratch_shapes=[pltpu.VMEM((count, T, 384), BF), pltpu.SemaphoreType.DMA((count,))],
        input_output_aliases={} if hidden is None else {len(args) - 1: 0},
    )(*args)


def join(parts, place, got, own6, hidden):
    args = [place, *got, *own6, hidden]
    count = sum(len(PARTS[p]) * STEPS[p] for p in parts) + (G if own6 else 0)
    stage = [pltpu.VMEM((G, T, B), F32), pltpu.VMEM((G, T, B), BF)] if own6 else []
    return call(
        functools.partial(join_kernel, parts, bool(own6)),
        [(hidden.shape, BF)],
        [SMEM] + [VMEM] * (len(args) - 2) + [ANY],
        [ANY],
        "join_" + parts[-1],
        scratch_shapes=stage + [pltpu.SemaphoreType.DMA((count,))],
        input_output_aliases={len(args) - 1: 0},
    )(*args)[0]


def on_device(tokens, master, moment, second, old_cell, new_cell, regrown, new_rows):
    c = lax.axis_index("core")
    cell = lax.axis_index("z") * C + c
    place = jnp.stack([cell, c, lax.axis_index("x"), lax.axis_index("y")]).astype(jnp.int32)
    rows = new_rows.T
    old_cell, new_cell, regrown = old_cell.T, new_cell.T, regrown.T
    block, info = call(
        prep_kernel, [((1, B, B), BF), ((8,), jnp.int32)], [SMEM] * 4 + [VMEM], [VMEM, SMEM], "prep"
    )(place, old_cell, new_cell, regrown, master)
    own = lax.all_gather(block, "z", axis=0, tiled=True)
    other = to_sibling(own)
    (picked,) = call(pick_kernel, [((4, MINE, B, B), BF)], [SMEM, SMEM, VMEM, VMEM], [VMEM], "pick")(
        place, old_cell, own, other
    )
    picked, master, moment, second, tokens = lax.optimization_barrier((picked, master, moment, second, tokens))
    line = gather(picked, line_groups(True)).reshape(4 * MINE, B, B)
    theirs = to_sibling(tokens)
    load = jnp.concatenate([master, moment, second]).astype(BF)
    low = along_cells(load, 3)
    high = along_cells(load, -3)
    up, down = call(middle_kernel, [((3, B, B), BF)] * 2, [SMEM] + [VMEM] * 3, [VMEM] * 2, "middle")(
        info, load, low, high
    )
    line, up, down, theirs = lax.optimization_barrier((line, up, down, theirs))
    halves = [line[: 2 * MINE], line[2 * MINE :]]
    lower, upper = [along_ring(halves[0], 1)], [along_ring(halves[1], -1)]
    lower.append(along_ring(halves[1], 1))
    upper.insert(0, along_ring(halves[0], -1))
    below = along_cells(up, 1)
    above = along_cells(down, -1)
    over = [along_ring(lower[0], 1), along_ring(upper[1], -1)]
    tokens, below, above = lax.optimization_barrier((tokens, below, above))
    hidden, send, own6_early = product("early", place, rows, tokens, theirs, [*halves, *lower, *upper], None)
    send, over = lax.optimization_barrier((send, over))
    got_early = to_sibling(send)
    states = call(settle_kernel, [((1, B, B), F32)] * 3, [SMEM] + [VMEM] * 7, [VMEM] * 3, "settle")(
        info, master, moment, second, low, high, below, above
    )
    over, states = lax.optimization_barrier((over, tuple(states)))
    hidden, send, own6_opposite = product("opposite", place, rows, tokens, theirs, over, hidden)
    got_opposite = to_sibling(send)
    hidden = join(("early",), place, (got_early,), (), hidden)
    hidden = join(("opposite",), place, (got_early, got_opposite), (own6_early, own6_opposite), hidden)
    return (hidden, *states)


def solution(mesh):
    fine = Mesh(np.asarray(mesh.devices).reshape(X, Y, Z, C), ALL)
    return jax.shard_map(
        on_device,
        mesh=fine,
        in_specs=(P(ALL, None),) + (P(ALL, None, None),) * 3 + (P(("x", "y"), None),) * 3 + (P(),),
        out_specs=(P(ALL, None),) + (P(ALL, None, None),) * 3,
        check_vma=False,
    )
```

```python
import functools
import numpy as np
import jax
import jax.numpy as jnp
from jax import lax
from jax.experimental import pallas as pl
from jax.experimental.pallas import tpu as pltpu
from jax.sharding import Mesh, PartitionSpec as P

BF = jnp.bfloat16
F32 = jnp.float32
X, Y, Z, C = 4, 4, 16, 2
G = X * Y
B = 128
COLS = 7
K = 4
MINE = 14
T = 128
ALL = ("x", "y", "z", "core")
VMEM = pl.BlockSpec(memory_space=pltpu.VMEM)
SMEM = pl.BlockSpec(memory_space=pltpu.SMEM)
ANY = pl.BlockSpec(memory_space=pl.ANY)
PARAMS = pltpu.CompilerParams(vmem_limit_bytes=48 << 20)


def device(x, y, z, c):
    return ((x * Y + y) * Z + z) * C + c


def line_groups(first):
    out = []
    for c in range(C):
        for z in range(Z):
            for o in range(4):
                along_x = (c == 0) == first
                out.append([device(i, o, z, c) if along_x else device(o, i, z, c) for i in range(4)])
    return out


PARTS = {
    "early": ((0, 0), (0, 2), (3, 0), (3, 2), (1, 0), (1, 2)),
    "opposite": ((2, 0), (2, 2)),
}
STEPS = {"early": 2, "opposite": 2}


def group_at(place, c, shift, q):
    line = (jnp.where(c == 0, place[3], place[2]) + shift) % 4
    return jnp.where(c == 0, q * 4 + line, line * 4 + q)


def prep_kernel(place, slots, master, block, info):
    cell = place[0]
    above, below = (cell + 1) % (Z * C), (cell - 1) % (Z * C)

    def look(s, carry):
        kept, o0, k0, op, om = carry
        packed = slots[s % K, s // K]
        o, n, r = packed % 32, packed // 32 % 32, packed // 1024
        kept = jnp.where((o == cell) & (r == 0), 1, kept)
        k0 = jnp.where((n == cell) & (r == 0), 1, k0)
        o0 = jnp.where(n == cell, o, o0)
        op = jnp.where(n == above, o, op)
        om = jnp.where(n == below, o, om)
        return kept, o0, k0, op, om

    kept, o0, k0, op, om = lax.fori_loop(
        0, COLS * K, look, (jnp.int32(0), cell, jnp.int32(0), above, below), unroll=True
    )

    def split(d):
        a = (d + 1 > 1).astype(jnp.int32) * (d > 1).astype(jnp.int32) - (d < -1).astype(jnp.int32)
        return a, d - 3 * a

    a0, b0 = split(cell - o0)
    ap, _ = split(above - op)
    am, _ = split(below - om)
    info[0] = k0
    info[1] = a0
    info[2] = b0
    info[3] = ap
    info[4] = am
    block[0] = jnp.where(kept == 1, master[0], 0.0).astype(BF)


def middle_kernel(info, own, low, high, up, down):
    for out, at in ((up, 3), (down, 4)):
        a = info[at]
        out[...] = jnp.where(a == 0, own[...], jnp.where(a == 1, low[...], high[...]))


def settle_kernel(info, master, moment, second, low, high, below, above, *outs):
    keep, a, b = info[0], info[1], info[2]
    for m, (own, out) in enumerate(zip((master, moment, second), outs)):
        same = jnp.where(a == 0, own[0], jnp.where(a == 1, low[m], high[m]).astype(F32))
        moved = jnp.where(b == 1, below[m], above[m]).astype(F32)
        value = jnp.where(b == 0, same, moved)
        out[0] = jnp.where(keep == 1, value, 0.0)


def pick_kernel(place, slots, own, other, out):
    c = place[1]
    for j in range(MINE):
        if j < 12:
            o = slots[j % K, 3 * c + j // K] % 32
        else:
            o = slots[2 * c + j - 12, COLS - 1] % 32
        at = o // 2
        block = jnp.where(o % 2 == c, own[at], other[at])
        for t in range(4):
            out[t, j] = block


def product_kernel(part, place, rows, mine, theirs, *refs):
    layout, steps = PARTS[part], STEPS[part]
    given, refs = refs[: len(layout)], refs[len(layout) :]
    hidden, send, own6, stage, sem = refs[-5:]
    c = place[1]
    step = pl.program_id(0)

    def copy_out(n, s):
        shift, first = layout[n]
        i = n * steps + s
        col = group_at(place, c, shift, first + s) * COLS + 3 * c
        to = hidden.at[:, pl.ds(pl.multiple_of(col * B, B), 3 * B)]
        return pltpu.make_async_copy(stage.at[i], to, sem.at[i])

    for n, (shift, first) in enumerate(layout):
        i = n * steps + step
        f = group_at(place, c, shift, first + step)
        for j in range(4):
            col = f * COLS + (3 * c + j if j < 3 else COLS - 1)
            count = K if j < 3 else 2
            ks = [k if j < 3 else 2 * c + k for k in range(count)]
            at = [pl.multiple_of(rows[k, col] * B, B) for k in ks]
            left = jnp.concatenate(
                [jnp.concatenate([ref[:, pl.ds(p, B)] for p in at], axis=1) for ref in (mine, theirs)], axis=0
            )
            right = given[n][j * K : j * K + count].reshape(count * B, B)
            acc = jnp.dot(left, right, preferred_element_type=F32)
            if j < 3:
                stage[i, :, j * B : j * B + B] = acc[:T].astype(BF)
            else:
                own6[i] = acc[:T]
            send[:, pl.ds(pl.multiple_of(i * 512 + j * B, B), B)] = acc[T:].astype(BF)
        copy_out(n, step).start()

    @pl.when(step == steps - 1)
    def _():
        for n in range(len(layout)):
            for s in range(steps):
                copy_out(n, s).wait()


def join_kernel(parts, last, *refs):
    refs = list(refs)
    place = refs.pop(0)
    got = {part: refs.pop(0) for part in (PARTS if last else parts)}
    own6 = {part: refs.pop(0) for part in PARTS} if last else {}
    refs.pop(0)
    hidden = refs.pop(0)
    sem = refs.pop()
    c = place[1]

    def items(part):
        for n, (shift, first) in enumerate(PARTS[part]):
            for s in range(STEPS[part]):
                yield n * STEPS[part] + s, shift, first + s

    copies = []

    def put(source, f, col, width):
        to = hidden.at[:, pl.ds(pl.multiple_of((f * COLS + col) * B, B), width)]
        copies.append(pltpu.make_async_copy(source, to, sem.at[len(copies)]))
        copies[-1].start()

    for part in parts:
        for i, shift, q in items(part):
            put(got[part].at[:, i * 512 : i * 512 + 384], group_at(place, 1 - c, shift, q), 3 * (1 - c), 384)
    if last:
        total, stage = refs
        for part in PARTS:
            for i, shift, q in items(part):
                total[group_at(place, c, shift, q)] = own6[part][i]
        for part in PARTS:
            for i, shift, q in items(part):
                f = group_at(place, 1 - c, shift, q)
                stage[f] = (total[f] + got[part][:, i * 512 + 384 : i * 512 + 512].astype(F32)).astype(BF)
                put(stage.at[f], f, COLS - 1, B)
    for copy in copies:
        copy.wait()


def gather(blocks, groups):
    return lax.all_to_all(blocks, ALL, 0, 0, tiled=True, axis_index_groups=groups)


def along_ring(value, distance):
    route = [(ring[i], ring[(i + distance) % 4]) for ring in line_groups(False) for i in range(4)]
    return lax.ppermute(value, ALL, route)


def to_sibling(value):
    return lax.ppermute(value, "core", [(0, 1), (1, 0)])


def along_cells(value, distance):
    route = [(i, (i + distance) % (Z * C)) for i in range(Z * C)]
    return lax.ppermute(value, ("z", "core"), route)


def call(kernel, shapes, in_specs, out_specs, name, **more):
    out = [jax.ShapeDtypeStruct(s, d) for s, d in shapes]
    return pl.pallas_call(
        kernel, out_shape=out, in_specs=in_specs, out_specs=out_specs, name=name, compiler_params=PARAMS, **more
    )


def product(part, place, rows, mine, theirs, given, hidden):
    count = len(given) * STEPS[part]
    whole = lambda s: pl.BlockSpec(s, lambda g: (0,) * len(s))
    args = [place, rows, mine, theirs, *given] + ([] if hidden is None else [hidden])
    return call(
        functools.partial(product_kernel, part),
        [((T, G * COLS * B), BF), ((T, count * 512), BF), ((count, T, B), F32)],
        [SMEM, SMEM, whole(mine.shape), whole(theirs.shape)]
        + [pl.BlockSpec((MINE, B, B), lambda g: (g, 0, 0))] * len(given)
        + ([] if hidden is None else [ANY]),
        [ANY, whole((T, count * 512)), whole((count, T, B))],
        "product_" + part,
        grid=(STEPS[part],),
        cost_estimate=pl.CostEstimate(
            flops=count * MINE * 2 * B * B * 2 * T, bytes_accessed=count * (MINE * B * B * 2 + T * B * 20), transcendentals=0
        ),
        scratch_shapes=[pltpu.VMEM((count, T, 384), BF), pltpu.SemaphoreType.DMA((count,))],
        input_output_aliases={} if hidden is None else {len(args) - 1: 0},
    )(*args)


def join(parts, place, got, own6, hidden):
    args = [place, *got, *own6, hidden]
    count = sum(len(PARTS[p]) * STEPS[p] for p in parts) + (G if own6 else 0)
    stage = [pltpu.VMEM((G, T, B), F32), pltpu.VMEM((G, T, B), BF)] if own6 else []
    return call(
        functools.partial(join_kernel, parts, bool(own6)),
        [(hidden.shape, BF)],
        [SMEM] + [VMEM] * (len(args) - 2) + [ANY],
        [ANY],
        "join_" + parts[-1],
        scratch_shapes=stage + [pltpu.SemaphoreType.DMA((count,))],
        input_output_aliases={len(args) - 1: 0},
    )(*args)[0]


def on_device(tokens, master, moment, second, old_cell, new_cell, regrown, new_rows):
    c = lax.axis_index("core")
    cell = lax.axis_index("z") * C + c
    place = jnp.stack([cell, c, lax.axis_index("x"), lax.axis_index("y")]).astype(jnp.int32)
    rows = new_rows.T
    slots = old_cell.T + 32 * new_cell.T + 1024 * (regrown.T != 0).astype(jnp.int32)
    block, info = call(
        prep_kernel, [((1, B, B), BF), ((8,), jnp.int32)], [SMEM] * 2 + [VMEM], [VMEM, SMEM], "prep"
    )(place, slots, master)
    own = lax.all_gather(block, "z", axis=0, tiled=True)
    own, tokens = lax.optimization_barrier((own, tokens))
    other = to_sibling(own)
    theirs = to_sibling(tokens)
    (picked,) = call(pick_kernel, [((4, MINE, B, B), BF)], [SMEM, SMEM, VMEM, VMEM], [VMEM], "pick")(
        place, slots, own, other
    )
    picked, master, moment, second, theirs = lax.optimization_barrier((picked, master, moment, second, theirs))
    line = gather(picked, line_groups(True)).reshape(4 * MINE, B, B)
    load = jnp.concatenate([master, moment, second]).astype(BF)
    low = along_cells(load, 3)
    high = along_cells(load, -3)
    up, down = call(middle_kernel, [((3, B, B), BF)] * 2, [SMEM] + [VMEM] * 3, [VMEM] * 2, "middle")(
        info, load, low, high
    )
    line, up, down = lax.optimization_barrier((line, up, down))
    halves = [line[: 2 * MINE], line[2 * MINE :]]
    lower, upper = [along_ring(halves[0], 1)], [along_ring(halves[1], -1)]
    lower.append(along_ring(halves[1], 1))
    upper.insert(0, along_ring(halves[0], -1))
    below = along_cells(up, 1)
    above = along_cells(down, -1)
    over = [along_ring(lower[0], 1), along_ring(upper[1], -1)]
    tokens, below, above = lax.optimization_barrier((tokens, below, above))
    hidden, send, own6_early = product("early", place, rows, tokens, theirs, [*halves, *lower, *upper], None)
    send, over = lax.optimization_barrier((send, over))
    got_early = to_sibling(send)
    states = call(settle_kernel, [((1, B, B), F32)] * 3, [SMEM] + [VMEM] * 7, [VMEM] * 3, "settle")(
        info, master, moment, second, low, high, below, above
    )
    hidden, send, own6_opposite = product("opposite", place, rows, tokens, theirs, over, hidden)
    got_opposite = to_sibling(send)
    hidden = join(("early", "opposite"), place, (got_early, got_opposite), (own6_early, own6_opposite), hidden)
    return (hidden, *states)


def solution(mesh):
    fine = Mesh(np.asarray(mesh.devices).reshape(X, Y, Z, C), ALL)
    return jax.shard_map(
        on_device,
        mesh=fine,
        in_specs=(P(ALL, None),) + (P(ALL, None, None),) * 3 + (P(("x", "y"), None),) * 3 + (P(),),
        out_specs=(P(ALL, None),) + (P(ALL, None, None),) * 3,
        check_vma=False,
    )
```

```python
import functools
import numpy as np
import jax
import jax.numpy as jnp
from jax import lax
from jax.experimental import pallas as pl
from jax.experimental.pallas import tpu as pltpu
from jax.sharding import Mesh, PartitionSpec as P

BF = jnp.bfloat16
F32 = jnp.float32
X, Y, Z, C = 4, 4, 16, 2
G = X * Y
B = 128
COLS = 7
K = 4
MINE = 14
T = 128
ALL = ("x", "y", "z", "core")
VMEM = pl.BlockSpec(memory_space=pltpu.VMEM)
SMEM = pl.BlockSpec(memory_space=pltpu.SMEM)
ANY = pl.BlockSpec(memory_space=pl.ANY)
PARAMS = pltpu.CompilerParams(vmem_limit_bytes=48 << 20)


def device(x, y, z, c):
    return ((x * Y + y) * Z + z) * C + c


def line_groups(first):
    out = []
    for c in range(C):
        for z in range(Z):
            for o in range(4):
                along_x = (c == 0) == first
                out.append([device(i, o, z, c) if along_x else device(o, i, z, c) for i in range(4)])
    return out


PARTS = {
    "early": ((0, 0), (0, 2), (3, 0), (3, 2), (1, 0), (1, 2)),
    "opposite": ((2, 0), (2, 2)),
}
STEPS = {"early": 2, "opposite": 2}


def group_at(place, c, shift, q):
    line = (jnp.where(c == 0, place[3], place[2]) + shift) % 4
    return jnp.where(c == 0, q * 4 + line, line * 4 + q)


def prep_kernel(place, slots, master, block, info):
    cell = place[0]
    above, below = (cell + 1) % (Z * C), (cell - 1) % (Z * C)

    def look(s, carry):
        kept, o0, k0, op, om = carry
        packed = slots[s % K, s // K]
        o, n, r = packed & 31, (packed >> 5) & 31, packed >> 10
        kept = jnp.where((o == cell) & (r == 0), 1, kept)
        k0 = jnp.where((n == cell) & (r == 0), 1, k0)
        o0 = jnp.where(n == cell, o, o0)
        op = jnp.where(n == above, o, op)
        om = jnp.where(n == below, o, om)
        return kept, o0, k0, op, om

    kept, o0, k0, op, om = lax.fori_loop(
        0, COLS * K, look, (jnp.int32(0), cell, jnp.int32(0), above, below), unroll=True
    )

    def split(d):
        a = (d + 1 > 1).astype(jnp.int32) * (d > 1).astype(jnp.int32) - (d < -1).astype(jnp.int32)
        return a, d - 3 * a

    a0, b0 = split(cell - o0)
    ap, _ = split(above - op)
    am, _ = split(below - om)
    info[0] = k0
    info[1] = a0
    info[2] = b0
    info[3] = ap
    info[4] = am
    block[0] = jnp.where(kept == 1, master[0], 0.0).astype(BF)


def middle_kernel(info, own, low, high, up, down):
    for out, at in ((up, 3), (down, 4)):
        a = info[at]
        out[...] = jnp.where(a == 0, own[...], jnp.where(a == 1, low[...], high[...]))


def settle_kernel(info, master, moment, second, low, high, below, above, *outs):
    keep, a, b = info[0], info[1], info[2]
    for m, (own, out) in enumerate(zip((master, moment, second), outs)):
        same = jnp.where(a == 0, own[0], jnp.where(a == 1, low[m], high[m]).astype(F32))
        moved = jnp.where(b == 1, below[m], above[m]).astype(F32)
        value = jnp.where(b == 0, same, moved)
        out[0] = jnp.where(keep == 1, value, 0.0)


def pick_kernel(place, slots, own, other, out):
    c = place[1]
    for j in range(MINE):
        if j < 12:
            o = slots[j % K, 3 * c + j // K] & 31
        else:
            o = slots[2 * c + j - 12, COLS - 1] & 31
        at = o >> 1
        block = jnp.where((o & 1) == c, own[at], other[at])
        for t in range(4):
            out[t, j] = block


def product_kernel(part, place, rows, mine, theirs, *refs):
    layout, steps = PARTS[part], STEPS[part]
    given, refs = refs[: len(layout)], refs[len(layout) :]
    hidden, send, own6, stage, sem = refs[-5:]
    c = place[1]
    step = pl.program_id(0)

    def copy_out(n, s):
        shift, first = layout[n]
        i = n * steps + s
        col = group_at(place, c, shift, first + s) * COLS + 3 * c
        to = hidden.at[:, pl.ds(pl.multiple_of(col * B, B), 3 * B)]
        return pltpu.make_async_copy(stage.at[i], to, sem.at[i])

    for n, (shift, first) in enumerate(layout):
        i = n * steps + step
        f = group_at(place, c, shift, first + step)
        for j in range(4):
            col = f * COLS + (3 * c + j if j < 3 else COLS - 1)
            count = K if j < 3 else 2
            ks = [k if j < 3 else 2 * c + k for k in range(count)]
            at = [pl.multiple_of(rows[k, col] * B, B) for k in ks]
            left = jnp.concatenate(
                [jnp.concatenate([ref[:, pl.ds(p, B)] for p in at], axis=1) for ref in (mine, theirs)], axis=0
            )
            right = given[n][j * K : j * K + count].reshape(count * B, B)
            acc = jnp.dot(left, right, preferred_element_type=F32)
            if j < 3:
                stage[i, :, j * B : j * B + B] = acc[:T].astype(BF)
            else:
                own6[i] = acc[:T]
            send[:, pl.ds(pl.multiple_of(i * 512 + j * B, B), B)] = acc[T:].astype(BF)
        copy_out(n, step).start()

    @pl.when(step == steps - 1)
    def _():
        for n in range(len(layout)):
            for s in range(steps):
                copy_out(n, s).wait()


def join_kernel(parts, last, *refs):
    refs = list(refs)
    place = refs.pop(0)
    got = {part: refs.pop(0) for part in (PARTS if last else parts)}
    own6 = {part: refs.pop(0) for part in PARTS} if last else {}
    refs.pop(0)
    hidden = refs.pop(0)
    sem = refs.pop()
    c = place[1]

    def items(part):
        for n, (shift, first) in enumerate(PARTS[part]):
            for s in range(STEPS[part]):
                yield n * STEPS[part] + s, shift, first + s

    copies = []

    def put(source, f, col, width):
        to = hidden.at[:, pl.ds(pl.multiple_of((f * COLS + col) * B, B), width)]
        copies.append(pltpu.make_async_copy(source, to, sem.at[len(copies)]))
        copies[-1].start()

    for part in parts:
        for i, shift, q in items(part):
            put(got[part].at[:, i * 512 : i * 512 + 384], group_at(place, 1 - c, shift, q), 3 * (1 - c), 384)
    if last:
        total, stage = refs
        for part in PARTS:
            for i, shift, q in items(part):
                total[group_at(place, c, shift, q)] = own6[part][i]
        for part in PARTS:
            for i, shift, q in items(part):
                f = group_at(place, 1 - c, shift, q)
                stage[f] = (total[f] + got[part][:, i * 512 + 384 : i * 512 + 512].astype(F32)).astype(BF)
                put(stage.at[f], f, COLS - 1, B)
    for copy in copies:
        copy.wait()


def gather(blocks, groups):
    return lax.all_to_all(blocks, ALL, 0, 0, tiled=True, axis_index_groups=groups)


def along_ring(value, distance):
    route = [(ring[i], ring[(i + distance) % 4]) for ring in line_groups(False) for i in range(4)]
    return lax.ppermute(value, ALL, route)


def to_sibling(value):
    return lax.ppermute(value, "core", [(0, 1), (1, 0)])


def along_cells(value, distance):
    route = [(i, (i + distance) % (Z * C)) for i in range(Z * C)]
    return lax.ppermute(value, ("z", "core"), route)


def call(kernel, shapes, in_specs, out_specs, name, **more):
    out = [jax.ShapeDtypeStruct(s, d) for s, d in shapes]
    return pl.pallas_call(
        kernel, out_shape=out, in_specs=in_specs, out_specs=out_specs, name=name, compiler_params=PARAMS, **more
    )


def product(part, place, rows, mine, theirs, given, hidden):
    count = len(given) * STEPS[part]
    whole = lambda s: pl.BlockSpec(s, lambda g: (0,) * len(s))
    args = [place, rows, mine, theirs, *given] + ([] if hidden is None else [hidden])
    return call(
        functools.partial(product_kernel, part),
        [((T, G * COLS * B), BF), ((T, count * 512), BF), ((count, T, B), F32)],
        [SMEM, SMEM, whole(mine.shape), whole(theirs.shape)]
        + [pl.BlockSpec((MINE, B, B), lambda g: (g, 0, 0))] * len(given)
        + ([] if hidden is None else [ANY]),
        [ANY, whole((T, count * 512)), whole((count, T, B))],
        "product_" + part,
        grid=(STEPS[part],),
        cost_estimate=pl.CostEstimate(
            flops=count * MINE * 2 * B * B * 2 * T, bytes_accessed=count * (MINE * B * B * 2 + T * B * 20), transcendentals=0
        ),
        scratch_shapes=[pltpu.VMEM((count, T, 384), BF), pltpu.SemaphoreType.DMA((count,))],
        input_output_aliases={} if hidden is None else {len(args) - 1: 0},
    )(*args)


def join(parts, place, got, own6, hidden):
    args = [place, *got, *own6, hidden]
    count = sum(len(PARTS[p]) * STEPS[p] for p in parts) + (G if own6 else 0)
    stage = [pltpu.VMEM((G, T, B), F32), pltpu.VMEM((G, T, B), BF)] if own6 else []
    return call(
        functools.partial(join_kernel, parts, bool(own6)),
        [(hidden.shape, BF)],
        [SMEM] + [VMEM] * (len(args) - 2) + [ANY],
        [ANY],
        "join_" + parts[-1],
        scratch_shapes=stage + [pltpu.SemaphoreType.DMA((count,))],
        input_output_aliases={len(args) - 1: 0},
    )(*args)[0]


def on_device(tokens, master, moment, second, old_cell, new_cell, regrown, new_rows):
    c = lax.axis_index("core")
    cell = lax.axis_index("z") * C + c
    place = jnp.stack([cell, c, lax.axis_index("x"), lax.axis_index("y")]).astype(jnp.int32)
    rows = new_rows.T
    slots = old_cell.T + 32 * new_cell.T + 1024 * (regrown.T != 0).astype(jnp.int32)
    block, info = call(
        prep_kernel, [((1, B, B), BF), ((8,), jnp.int32)], [SMEM] * 2 + [VMEM], [VMEM, SMEM], "prep"
    )(place, slots, master)
    own = lax.all_gather(block, "z", axis=0, tiled=True)
    own, tokens = lax.optimization_barrier((own, tokens))
    other = to_sibling(own)
    theirs = to_sibling(tokens)
    (picked,) = call(pick_kernel, [((4, MINE, B, B), BF)], [SMEM, SMEM, VMEM, VMEM], [VMEM], "pick")(
        place, slots, own, other
    )
    picked, master, moment, second = lax.optimization_barrier((picked, master, moment, second))
    line = gather(picked, line_groups(True)).reshape(4 * MINE, B, B)
    load = jnp.concatenate([master, moment, second]).astype(BF)
    low = along_cells(load, 3)
    high = along_cells(load, -3)
    up, down = call(middle_kernel, [((3, B, B), BF)] * 2, [SMEM] + [VMEM] * 3, [VMEM] * 2, "middle")(
        info, load, low, high
    )
    up, down, theirs = lax.optimization_barrier((up, down, theirs))
    line, up, down = lax.optimization_barrier((line, up, down))
    halves = [line[: 2 * MINE], line[2 * MINE :]]
    lower, upper = [along_ring(halves[0], 1)], [along_ring(halves[1], -1)]
    lower.append(along_ring(halves[1], 1))
    upper.insert(0, along_ring(halves[0], -1))
    below = along_cells(up, 1)
    above = along_cells(down, -1)
    over = [along_ring(lower[0], 1), along_ring(upper[1], -1)]
    tokens, below, above = lax.optimization_barrier((tokens, below, above))
    hidden, send, own6_early = product("early", place, rows, tokens, theirs, [*halves, *lower, *upper], None)
    send, over = lax.optimization_barrier((send, over))
    got_early = to_sibling(send)
    states = call(settle_kernel, [((1, B, B), F32)] * 3, [SMEM] + [VMEM] * 7, [VMEM] * 3, "settle")(
        info, master, moment, second, low, high, below, above
    )
    hidden, send, own6_opposite = product("opposite", place, rows, tokens, theirs, over, hidden)
    got_opposite = to_sibling(send)
    hidden = join(("early", "opposite"), place, (got_early, got_opposite), (own6_early, own6_opposite), hidden)
    return (hidden, *states)


def solution(mesh):
    fine = Mesh(np.asarray(mesh.devices).reshape(X, Y, Z, C), ALL)
    return jax.shard_map(
        on_device,
        mesh=fine,
        in_specs=(P(ALL, None),) + (P(ALL, None, None),) * 3 + (P(("x", "y"), None),) * 3 + (P(),),
        out_specs=(P(ALL, None),) + (P(ALL, None, None),) * 3,
        check_vma=False,
    )
```
